32 devices in a mesh: walk: 2 (over y), row: 4 (over x, core), col: 4 (over z).
Axes of the slice: x: 2, y: 2, z: 4, core: 2. Of those that a mesh axis runs over, the one named last changes fastest.
Arguments:
- states: bfloat16 [2048, 512], P(('walk', 'row'), 'col'), parts along dimension 0, may hold values from -6 to 6
- spin: int32 [2048], P('walk'), parts along dimension 0, may hold values 0 or 1
- shift: int32 [32, 16], P('walk'), parts along dimension 0, may hold values from 0 to 26
- w_left: bfloat16 [2, 512, 512], replicated, may hold values from -0.25 to 0.25
- w_right: bfloat16 [2, 512, 512], replicated, may hold values from -0.25 to 0.25
- w_out: bfloat16 [2, 512, 512], replicated, may hold values from -0.25 to 0.25
- out_bias: float32 [2, 512], replicated, may hold values from -3 to 3
- shift_table: float32 [27, 512], replicated, may hold values from -6 to 6
- same_bias: float32 [512], replicated, may hold values from -6 to 6
- w_orbital: bfloat16 [512, 1024], P(None, 'col'), may hold values from -0.25 to 0.25
- envelope: float32 [2048, 1024], P(('walk', 'row'), 'col'), parts along dimension 0, may hold values from 0.05 to 0.5
- approx_inverse: float32 [2048, 1024], P(('walk', 'row'), 'col'), parts along dimension 0, may hold values from -0.1875 to 0.1875
Outputs:
- new_states: bfloat16 [2048, 512], P(('walk', 'row'), 'col'), parts along dimension 0
- refined: float32 [2048, 1024], P(('walk', 'row'), 'col'), parts along dimension 0
The draws below stay inside these ranges and needn't reach their ends.
There are 2 independent parts, one for each index of `walk`. The reference program is written for one: setup_inputs(seed, part) draws one part's arguments, and reference() takes and returns one part's arrays. A program takes and returns all parts, laid end to end along the dimension named above; an argument that names none is the same for every part. Nothing has to cross between parts.
Inputs may be any that keep to these rules, and one draw needn't show every extreme that they name: `shift`: indices into shift_table.
All inputs are finite; a program needn't handle non-finite values.
Results may differ from the reference program's by a relative error of at most 0.0047.
Values may be sent and summed in bfloat16 or wider, within the bound.
No kernel may reach another device: no remote copies, remote signals or barrier semaphores. Data moves between devices by JAX's collectives and lax.ppermute only.
A program may use at most 64 MiB of HBM per device.

```python
import math
import jax
import jax.numpy as jnp
from jax import lax

N = 1024
W = 512
H = 512
NB = 16
S = 27
LAYERS = 2


def plant(values, stream_key, smallest, high):
    dims = values.shape
    spot = [jax.random.randint(jax.random.fold_in(stream_key, axis), (), 0, dims[axis]) for axis in range(len(dims))]
    values = values.at[tuple(spot)].set(smallest)
    longest = dims.index(max(dims))
    spot[longest] = (spot[longest] + 1) % dims[longest]
    return values.at[tuple(spot)].set(high)


def block_scale(stream_key, extent, cuts, least, largest):
    def one(dim, shards_of):
        steps = jax.random.uniform(jax.random.fold_in(jax.random.fold_in(stream_key, 6), dim), (shards_of,), jnp.float32, least / len(cuts), largest / len(cuts))
        return jnp.repeat(jnp.exp(steps), extent[dim] // shards_of).reshape((-1,) + (1,) * (len(extent) - dim - 1))

    gain = one(*cuts[0])
    for cut in cuts[1:]:
        gain = gain * one(*cut)
    return gain


def bell_draw(key, dims, scale, bound, shards=(), held_as=jnp.bfloat16):
    factor_of = block_scale(key, dims, shards, -0.22, 0.18) if shards else 1.0
    result = jax.random.normal(key, dims, jnp.float32) * scale * factor_of
    return jnp.minimum(jnp.maximum(result, -bound), bound).astype(held_as)


def setup_inputs(seed: int = 0, part: int = 0) -> dict:
    key_of = jax.random.split(jax.random.key(seed), 13)
    part_splits = jax.random.split(jax.random.fold_in(key_of[12], part), 13)
    return {
        "states": bell_draw(part_splits[0], (N, W), 1.0, 6.0, ((0, 4), (1, 4))),
        "spin": plant((jax.random.randint(part_splits[1], (N,), 0, 2) < 1).astype(jnp.int32), jax.random.fold_in(part_splits[1], 1), 0, 1),
        "shift": plant(jax.random.randint(part_splits[2], (NB, NB), 0, S), jax.random.fold_in(part_splits[2], 1), 0, S - 1).astype(jnp.int32),
        "w_left": bell_draw(key_of[3], (LAYERS, W, H), W ** -0.5, 0.25),
        "w_right": bell_draw(key_of[4], (LAYERS, W, H), W ** -0.5, 0.25),
        "w_out": bell_draw(key_of[5], (LAYERS, H, W), H ** -0.5, 0.25),
        "out_bias": bell_draw(key_of[6], (LAYERS, W), 0.5, 3.0, (), jnp.float32),
        "shift_table": bell_draw(key_of[7], (S, H), 1.0, 6.0, (), jnp.float32),
        "same_bias": bell_draw(key_of[8], (H,), 1.0, 6.0, (), jnp.float32),
        "w_orbital": bell_draw(key_of[9], (W, N), W ** -0.5, 0.25, ((1, 4),)),
        "envelope": jnp.clip(jnp.exp(math.log(0.5) - 2.3025851 * jax.random.uniform(part_splits[10], (N, N), jnp.float32) ** block_scale(part_splits[10], (N, N), ((0, 4), (1, 4)), -0.2, 0.2)), 0.05, 0.5),
        "approx_inverse": bell_draw(part_splits[11], (N, N), N ** -0.5, 0.1875, ((0, 4), (1, 4)), jnp.float32),
    }


def reference(states, spin, shift, w_left, w_right, w_out, out_bias, shift_table, same_bias, w_orbital, envelope, approx_inverse):
    block_size = N // NB
    onehot = (shift[:, :, None] == jnp.arange(S, dtype=jnp.int32)[None, None, :]).astype(jnp.float32)
    embedded = jnp.einsum("abs,sh->abh", onehot, shift_table, precision=lax.Precision.HIGHEST)
    same_spin = (spin[:, None] == spin[None, :]).astype(jnp.float32)
    hidden_state = states
    for layer_idx in range(LAYERS):
        left_part = jnp.dot(hidden_state, w_left[layer_idx], preferred_element_type=jnp.float32)
        right_part = jnp.dot(hidden_state, w_right[layer_idx], preferred_element_type=jnp.float32)
        weight_out = w_out[layer_idx].astype(jnp.float32)
        bias_out = out_bias[layer_idx]

        def row_messages(block_idx):
            begin_row = block_idx * block_size
            left_rows = lax.dynamic_slice_in_dim(left_part, begin_row, block_size, 0)
            same_rows = lax.dynamic_slice_in_dim(same_spin, begin_row, block_size, 0)
            shift_rows = jnp.repeat(embedded[block_idx], block_size, axis=0)
            pre_act = left_rows[:, None, :] + right_part[None, :, :] + shift_rows[None, :, :] + same_rows[:, :, None] * same_bias
            gated_vals = lax.optimization_barrier(jax.nn.silu(pre_act).astype(jnp.bfloat16)).astype(jnp.float32)
            message = jnp.tanh(jnp.einsum("ijh,hw->ijw", gated_vals, weight_out) + bias_out)
            return jnp.sum(message, axis=1) / N

        summed = lax.map(row_messages, jnp.arange(NB, dtype=jnp.int32))
        hidden_state = (hidden_state.astype(jnp.float32) + summed.reshape(N, -1)).astype(jnp.bfloat16)
    orbital = jnp.dot(hidden_state, w_orbital, preferred_element_type=jnp.float32) * envelope
    product = jnp.dot(orbital, approx_inverse, precision=lax.Precision.HIGHEST, preferred_element_type=jnp.float32)
    residual_part = 2.0 * jnp.eye(N, dtype=jnp.float32) - product
    refined = jnp.dot(approx_inverse, residual_part, precision=lax.Precision.HIGHEST, preferred_element_type=jnp.float32)
    return hidden_state, refined
```

```python
import functools
import math

import jax
import jax.numpy as jnp
from jax import lax
from jax.experimental import pallas as pl
from jax.experimental.pallas import tpu as pltpu
from jax.sharding import PartitionSpec as P


TILE = 64
AHEAD = 7
CHUNK = 1024
VMEM_LIMIT = 24 * 1024 * 1024
CODE = 64
F32 = jnp.float32
BF16 = jnp.bfloat16


def _vmem():
    return pl.BlockSpec(memory_space=pltpu.VMEM)


def _smem():
    return pl.BlockSpec(memory_space=pltpu.SMEM)


def tiling(per_chunk, senders):
    tile = math.gcd(TILE, senders)
    tiles = per_chunk * senders // tile
    slots = max(d for d in range(1, AHEAD + 2) if 2 * tiles % d == 0)
    return tile, tiles, slots


def pair_kernel(*refs, piece_rows, final, has_prev, count, rows, layers):
    senders = sum(piece_rows)
    pieces = refs[: len(piece_rows)]
    (own_ref, wl_ref, wr_ref, wo_ref, bias_ref, code_ref, spin_ref, table_ref, same_ref) = refs[
        len(piece_rows) : len(piece_rows) + 9
    ]
    wl_ref, wr_ref, wo_ref, bias_ref = (
        ref if layer is None else ref.at[layer] for ref, layer in zip((wl_ref, wr_ref, wo_ref, bias_ref), layers)
    )
    rest = list(refs[len(piece_rows) + 9 :])
    prev_ref = rest.pop(0) if has_prev else None
    res_ref = rest.pop(0) if final else None
    out_ref, left_ref, right_ref, gate_ref, sum_ref, bias8_ref, table2_ref = rest

    hidden = wl_ref.shape[1]
    half = hidden // 2
    per_chunk = gate_ref.shape[1] // senders
    chunks = rows // per_chunk
    tile, tiles, slots = tiling(per_chunk, senders)
    tiles_of = senders // tile
    ahead = slots - 1
    table = table_ref[...]
    table_hi = table.astype(BF16).astype(F32)
    table2_ref[: table.shape[0]] = table_hi.astype(BF16)
    table2_ref[table.shape[0] :] = (table - table_hi).astype(BF16)
    bias8_ref[...] = jnp.broadcast_to(bias_ref[...].reshape(1, -1), bias8_ref.shape)

    def first_layer(*accs):
        def staged(w_ref, n, k):
            pltpu.matmul_push_rhs(
                w_ref[k * half : (k + 1) * half, n * half : (n + 1) * half], staging_register=0, mxu_index=k
            )

        own_tiles = own_ref.shape[0] // 16
        for n in range(2):
            cols = slice(n * half, (n + 1) * half)
            for k in range(2):
                staged(wl_ref, n, k)
                for t in range(own_tiles):
                    pltpu.matmul_acc_lhs(
                        accs[2 * t + k],
                        own_ref[t * 16 : t * 16 + 16, k * half : (k + 1) * half],
                        0 if t == 0 else None,
                    )
            for t in range(own_tiles):
                left = 0.5 * (pltpu.matmul_pop(accs[2 * t]) + pltpu.matmul_pop(accs[2 * t + 1]))
                for i in range(t * 16, min(t * 16 + 16, rows)):
                    left_ref[i, :, cols] = jnp.broadcast_to(left[i - t * 16 : i - t * 16 + 1], (16, half)).astype(BF16)

    pl.run_scoped(first_layer, *[pltpu.ACC(k)((16, half), F32) for _ in range(own_ref.shape[0] // 16) for k in range(2)])

    size = math.gcd(TILE, *piece_rows)
    where = [(p, r) for p, n_rows in zip(pieces, piece_rows) for r in range(0, n_rows, size)]
    batch = 512 // size

    def second_layer(*accs):
        for first in range(0, len(where), batch):
            some = where[first : first + batch]
            hot = []
            codes = []
            for t in range(len(some)):
                code = code_ref[(first + t) * size : (first + t + 1) * size]
                spin = code // CODE
                which = code - spin * CODE
                one = which == lax.broadcasted_iota(jnp.int32, (size, table.shape[0]), 1)
                one = jnp.where(one, 1.0, 0.0).astype(BF16)
                hot.append(jnp.concatenate([one, one], axis=1))
                codes.append(spin)
            for n in range(2):
                cols = slice(n * half, (n + 1) * half)
                for k in range(2):
                    pltpu.matmul_push_rhs(
                        wr_ref[k * half : (k + 1) * half, cols], staging_register=0, mxu_index=k
                    )
                    for t, (piece, r) in enumerate(some):
                        pltpu.matmul_acc_lhs(
                            accs[2 * t + k], piece[r : r + size, k * half : (k + 1) * half], 0 if t == 0 else None
                        )
                pltpu.matmul_push_rhs(table2_ref[:, cols], staging_register=0, mxu_index=0)
                for t in range(len(some)):
                    pltpu.matmul_acc_lhs(accs[2 * t], hot[t], 0 if t == 0 else None)
                same = 0.5 * same_ref[:, cols]
                for t in range(len(some)):
                    right = 0.5 * (pltpu.matmul_pop(accs[2 * t]) + pltpu.matmul_pop(accs[2 * t + 1]))
                    at = (first + t) * size
                    for s in range(2):
                        right_ref[s, at : at + size, cols] = (right + jnp.where(codes[t] == s, same, 0.0)).astype(BF16)

    pl.run_scoped(second_layer, *[pltpu.ACC(k)((size, half), F32) for _ in range(min(batch, len(where))) for k in range(2)])

    piece_len = tile // 2

    def make(chunk, buf, step):
        pos = step * piece_len
        i = chunk * per_chunk + pos // senders
        j = pos % senders
        u = right_ref[spin_ref[i], j : j + piece_len, :] + jnp.tile(left_ref[i], (piece_len // 16, 1))
        gate_ref[buf, pos : pos + piece_len, :] = u + u * jnp.tanh(u)

    def push(n):
        for k in range(2):
            pltpu.matmul_push_rhs(
                wo_ref[k * half : (k + 1) * half, n * half : (n + 1) * half], staging_register=0, mxu_index=k
            )

    def run(*accs):
        def mm(buf, step, load):
            for k in range(2):
                pltpu.matmul_acc_lhs(
                    accs[2 * (step % slots) + k],
                    gate_ref[buf, (step % tiles) * tile : (step % tiles + 1) * tile, k * half : (k + 1) * half],
                    0 if load else None,
                )

        def pop(step):
            slot = 2 * (step % slots)
            return pltpu.matmul_pop(accs[slot]) + pltpu.matmul_pop(accs[slot + 1])

        for step in range(2 * tiles):
            make(0, 0, step)
        push(0)
        for step in range(ahead):
            mm(0, step, step == 0)

        def one_chunk(chunk, buf):
            following = jnp.minimum(chunk + 1, chunks - 1)
            total = None
            for step in range(2 * tiles):
                n = step // tiles
                if step % tiles == 0:
                    push(1 - n)
                make(following, 1 - buf, step)
                nxt = step + ahead
                mm(buf if nxt < 2 * tiles else 1 - buf, nxt, nxt % tiles == 0)
                m = jnp.tanh(pop(step) + jnp.tile(bias8_ref[:, n * half : (n + 1) * half], (tile // 8, 1)))
                m = m.reshape(tile // 8, 8, half)
                for q in range(tile // 8):
                    total = m[q] if total is None else total + m[q]
                if (step + 1) % tiles_of == 0:
                    i = chunk * per_chunk + (step % tiles) // tiles_of
                    sum_ref[i, :, n * half : (n + 1) * half] = total
                    total = None

        turn = 2 if chunks % 2 == 0 else 1

        def body(at, carry):
            for t in range(turn):
                chunk = turn * at + t
                one_chunk(chunk, t if turn == 2 else lax.rem(chunk, 2))
            return carry

        lax.fori_loop(0, chunks // turn, body, 0)
        for step in range(ahead):
            pop(step)

    pl.run_scoped(run, *[pltpu.ACC(k)((tile, half), F32) for _ in range(slots) for k in range(2)])

    summed = jnp.sum(sum_ref[...], axis=1)
    if has_prev:
        summed = summed + prev_ref[...]
    if final:
        out_ref[...] = (res_ref[...].astype(F32) + summed / count).astype(BF16)
    else:
        out_ref[...] = summed


def pair_call(pieces, own, wl, wr, wo, bias, code, spin, table, same, prev, res, count, layers, name):
    piece_rows = tuple(p.shape[0] for p in pieces)
    rows, senders = own.shape[0], sum(piece_rows)
    own = jnp.pad(own, ((0, -rows % 16), (0, 0)))
    hidden, width = wl.shape[-1], wo.shape[-1]
    per_chunk = max(d for d in range(1, rows + 1) if rows % d == 0 and (d == 1 or d * senders <= CHUNK))
    args = [*pieces, own, wl, wr, wo, bias, code, spin, table, same]
    specs = [_vmem()] * len(pieces) + [_vmem()] * 6 + [_smem()] + [_vmem()] * 2
    if prev is not None:
        args.append(prev)
        specs.append(_vmem())
    final = res is not None
    if final:
        args.append(res)
        specs.append(_vmem())
    pairs = rows * senders
    return pl.pallas_call(
        functools.partial(
            pair_kernel, piece_rows=piece_rows, final=final, has_prev=prev is not None, count=float(count), rows=rows,
            layers=layers,
        ),
        out_shape=jax.ShapeDtypeStruct((rows, width), BF16 if final else F32),
        in_specs=specs,
        out_specs=_vmem(),
        scratch_shapes=[
            pltpu.VMEM((rows, 16, hidden), BF16),
            pltpu.VMEM((2, senders, hidden), BF16),
            pltpu.VMEM((2, per_chunk * senders, hidden), BF16),
            pltpu.VMEM((rows, 8, width), F32),
            pltpu.VMEM((8, width), F32),
            pltpu.VMEM((2 * table.shape[0], hidden), BF16),
        ],
        cost_estimate=pl.CostEstimate(
            flops=2 * pairs * hidden * width, bytes_accessed=4 * hidden * width, transcendentals=pairs * (hidden + width)
        ),
        compiler_params=pltpu.CompilerParams(vmem_limit_bytes=VMEM_LIMIT),
        name=name,
    )(*args)


def newton_left_kernel(*refs, groups, rows_groups, half_index, with_states):
    col, row = lax.axis_index("col"), lax.axis_index("row")
    states_ref = refs[0]
    w_refs = refs[1 : 1 + groups]
    env_refs = refs[1 + groups : 1 + 2 * groups]
    x_refs = refs[1 + 2 * groups : 1 + 2 * groups + rows_groups]
    rest = list(refs[1 + 2 * groups + rows_groups :])
    first_ref = rest.pop(0) if with_states else None
    out_ref = rest.pop(0)
    new_ref = rest.pop(0) if with_states else None
    x_abs, sem = rest
    copies = [pltpu.make_async_copy(x_refs[q], x_abs.at[row ^ q], sem.at[q]) for q in range(rows_groups)]
    for copy in copies:
        copy.start()
    part = states_ref.shape[0] // groups
    features = new_ref.shape[3] if with_states else 0
    for s in range(groups if with_states else 0):
        for h, ref in enumerate((first_ref, states_ref)):
            new_ref[col ^ s, h] = ref[s * part : (s + 1) * part, pl.ds(pl.multiple_of(col * features, features), features)]
    orbitals = []
    for k in range(groups):
        env = jnp.concatenate(
            [
                env_refs[k][pl.ds(pl.multiple_of((col ^ s) * 2 * part + half_index * part, part), part), :]
                for s in range(groups)
            ],
            axis=0,
        )
        orbitals.append(jnp.dot(states_ref[...], w_refs[k][...], preferred_element_type=F32) * env)
    for copy in copies:
        copy.wait()
    total = None
    for k in range(groups):
        term = jnp.dot(
            orbitals[k], x_abs[col ^ k], preferred_element_type=F32, precision=lax.Precision.HIGHEST
        )
        total = term if total is None else total + term
    for s in range(groups):
        out_ref[col ^ s] = total[s * part : (s + 1) * part].astype(BF16)


def newton_left(states, w_parts, env_parts, x_parts, half_index, first, features, name):
    groups, rows_groups = len(w_parts), len(x_parts)
    part = states.shape[0] // groups
    width = x_parts[0].shape[1]
    any_spec = pl.BlockSpec(memory_space=pl.ANY)
    args = [states, *w_parts, *env_parts, *x_parts]
    specs = [_vmem()] * (1 + 2 * groups) + [any_spec] * rows_groups
    shapes = [jax.ShapeDtypeStruct((groups, part, width), BF16)]
    if first is not None:
        args.append(first)
        specs.append(_vmem())
        shapes.append(jax.ShapeDtypeStruct((groups, 2, part, features), BF16))
    return pl.pallas_call(
        functools.partial(
            newton_left_kernel,
            groups=groups,
            rows_groups=rows_groups,
            half_index=half_index,
            with_states=first is not None,
        ),
        out_shape=shapes,
        in_specs=specs,
        out_specs=[_vmem()] * len(shapes),
        scratch_shapes=[
            pltpu.VMEM((rows_groups, *x_parts[0].shape), F32),
            pltpu.SemaphoreType.DMA((rows_groups,)),
        ],
        compiler_params=pltpu.CompilerParams(vmem_limit_bytes=VMEM_LIMIT),
        cost_estimate=pl.CostEstimate(flops=1_000_000_000, bytes_accessed=3_000_000, transcendentals=0),
        name=name,
    )(*args)


def newton_right_kernel(*refs, groups, rows_groups):
    col, row = lax.axis_index("col"), lax.axis_index("row")
    first = refs[:rows_groups]
    second = refs[rows_groups : 2 * rows_groups]
    x_refs = refs[2 * rows_groups : 2 * rows_groups + groups]
    tile_ref, out_ref, x_abs, sem = refs[2 * rows_groups + groups :]
    copies = [pltpu.make_async_copy(x_refs[s], x_abs.at[col ^ s], sem.at[s]) for s in range(groups)]
    for copy in copies:
        copy.start()
    for copy in copies:
        copy.wait()
    total = 2.0 * tile_ref[...]
    for q in range(rows_groups):
        product = jnp.concatenate([first[q][...], second[q][...]], axis=1)
        product = product.reshape(-1, product.shape[2])
        total -= jnp.dot(x_abs[row ^ q], product, preferred_element_type=F32)
    out_ref[...] = total


def newton_right(first, second, x_parts, tile):
    groups, rows_groups = len(x_parts), len(first)
    any_spec = pl.BlockSpec(memory_space=pl.ANY)
    return pl.pallas_call(
        functools.partial(newton_right_kernel, groups=groups, rows_groups=rows_groups),
        out_shape=jax.ShapeDtypeStruct(tile.shape, F32),
        in_specs=[_vmem()] * (2 * rows_groups) + [any_spec] * groups + [_vmem()],
        out_specs=_vmem(),
        scratch_shapes=[
            pltpu.VMEM((groups, *x_parts[0].shape), BF16),
            pltpu.SemaphoreType.DMA((groups,)),
        ],
        compiler_params=pltpu.CompilerParams(vmem_limit_bytes=VMEM_LIMIT),
        name="newton_right",
    )(*first, *second, *x_parts, tile)


def exchange(x, axis):
    size = lax.axis_size(axis)
    return [x] + [lax.ppermute(x, axis, [(i, i ^ s) for i in range(size)]) for s in range(1, size)]


def xor_order(x, axis, index):
    size = x.shape[axis]
    bit = 1
    while bit < size:
        shape = x.shape[:axis] + (size // (2 * bit), 2, bit) + x.shape[axis + 1 :]
        flipped = jnp.flip(x.reshape(shape), axis=axis + 1).reshape(x.shape)
        x = jnp.where((index & bit) != 0, flipped, x)
        bit *= 2
    return x


def after(values, *events):
    out = lax.optimization_barrier((tuple(values), events))
    return list(out[0])


def newton_plain(states, new_rows, w_orbital, envelope, approx_inverse, row_begin, col_begin):
    count = approx_inverse.shape[0]
    orbital = jnp.dot(new_rows, w_orbital, preferred_element_type=F32) * envelope
    high = dict(precision=lax.Precision.HIGHEST, preferred_element_type=F32)
    panel = lax.all_gather(orbital, "col", axis=1, tiled=True)
    product = jnp.dot(panel, lax.all_gather(approx_inverse, "row", axis=0, tiled=True), **high)
    row_ids = row_begin + jnp.arange(count, dtype=jnp.int32)
    col_ids = col_begin + jnp.arange(approx_inverse.shape[1], dtype=jnp.int32)
    residual = 2.0 * (row_ids[:, None] == col_ids[None, :]).astype(F32) - product
    left = lax.all_gather(approx_inverse, "col", axis=1, tiled=True)
    return jnp.dot(left, lax.all_gather(residual, "row", axis=0, tiled=True), **high)


def per_device(
    states, spin, shift, w_left, w_right, w_out, out_bias, shift_table, same_bias, w_orbital, envelope, approx_inverse
):
    rows_n, cols_n = lax.axis_size("row"), lax.axis_size("col")
    row, col = lax.axis_index("row"), lax.axis_index("col")
    group = states.shape[0]
    count = group * rows_n
    mine = group // cols_n
    part = mine // 2
    block = count // shift.shape[0]
    layers = w_left.shape[0]
    features = states.shape[1]
    width = features * cols_n

    parts = exchange(states, "col")
    own_group = jnp.concatenate(parts, axis=1)
    near = [own_group, lax.ppermute(own_group, "row", [(i, i ^ 1) for i in range(rows_n)])]
    far = [lax.ppermute(own_group, "row", [(i, i ^ s) for i in range(rows_n)]) for s in range(2, rows_n)]

    table = jnp.pad(shift_table, ((0, 128 - shift_table.shape[0]), (0, 0)))
    same = same_bias[None, :]
    my_begin = row * group + col * mine
    my_spin = lax.dynamic_slice_in_dim(spin, my_begin, mine, 0)
    shift_row = lax.dynamic_slice_in_dim(shift, my_begin // block, 1, 0)[0]
    code = jnp.repeat(shift_row, block) + CODE * spin
    code = xor_order(code.reshape(rows_n, cols_n, 2, part), 0, row)
    code_first = code.reshape(count, 1)
    code_halves = [xor_order(code[:, :, h], 1, col).reshape(count // 2, 1) for h in range(2)]

    wl_first = xor_order(w_left[0].reshape(cols_n, features, -1), 0, col).reshape(width, -1)
    wr_first = xor_order(w_right[0].reshape(cols_n, features, -1), 0, col).reshape(width, -1)
    own_rel = lax.dynamic_slice_in_dim(own_group, col * mine, mine, 0)
    own_abs = jnp.concatenate(
        [p[:, None] for p in [lax.dynamic_slice_in_dim(q, col * mine, mine, 0) for q in parts]], axis=1
    )
    own_abs = xor_order(own_abs, 1, col).reshape(mine, width)

    near_n = 2 * group
    halves = [slice(0, part), slice(part, mine)]
    first = functools.partial(
        pair_call, wl=wl_first, wr=wr_first, wo=w_out, bias=out_bias, table=table, same=same, count=count,
        layers=(None, None, 0, 0),
    )
    partial_sum = first(near, own_rel, code=code_first[:near_n], spin=my_spin, prev=None, res=None, name="l0_near")
    state_halves = [
        first(
            far, own_rel[h], code=code_first[near_n:], spin=my_spin[h], prev=partial_sum[h], res=own_abs[h],
            name="l0_far",
        )
        for h in halves
    ]

    aligned = part % 16 == 0 and rows_n == cols_n
    w_parts = env_parts = x_col = x_row = None
    if aligned:
        w_orbital, envelope_late = after([w_orbital, envelope], own_group)
        w_parts = exchange(w_orbital, "col")
        env_parts = exchange(envelope_late, "col")
        (x_late,) = after([approx_inverse], partial_sum)
        x_col = exchange(x_late, "row")
        (x_late,) = after([approx_inverse], state_halves[1])
        x_row = exchange(x_late.astype(BF16), "col")

    for layer in range(1, layers):
        z = [jnp.concatenate(exchange(h, "col"), axis=0) for h in state_halves]
        others = [[lax.ppermute(g, "row", [(i, i ^ s) for i in range(rows_n)]) for s in range(1, rows_n)] for g in z]
        own = jnp.concatenate(state_halves, axis=0)
        call = functools.partial(
            pair_call, wl=w_left, wr=w_right, wo=w_out, bias=out_bias, table=table, same=same, count=count,
            layers=(layer,) * 4,
        )
        own_n = cols_n * part
        total = call([z[0]], own, code=code_halves[0][:own_n], spin=my_spin, prev=None, res=None, name="own_a")
        total = call(others[0], own, code=code_halves[0][own_n:], spin=my_spin, prev=total, res=None, name="other_a")
        total = call([z[1]], own, code=code_halves[1][:own_n], spin=my_spin, prev=total, res=None, name="own_b")
        state_halves = [
            call(
                others[1], own[h], code=code_halves[1][own_n:], spin=my_spin[h], prev=total[h], res=own[h],
                name="other_b",
            )
            for h in halves
        ]

    z = [jnp.concatenate(exchange(h, "col"), axis=0) for h in state_halves]
    if aligned:
        (p_first,) = newton_left(z[0], w_parts, env_parts, x_col, 0, None, features, "newton_a")
        p_second, new = newton_left(z[1], w_parts, env_parts, x_col, 1, z[0], features, "newton_b")
        refined = newton_right(exchange(p_first, "row"), exchange(p_second, "row"), x_row, approx_inverse)
        return new.reshape(group, features), refined
    rows_all = jnp.concatenate([g.reshape(cols_n, 1, part, width) for g in z], axis=1)
    rows_all = xor_order(rows_all, 0, col).reshape(group, width)
    new = lax.dynamic_slice_in_dim(rows_all, col * features, features, 1)
    return new, newton_plain(states, rows_all, w_orbital, envelope, approx_inverse, row * group, col * envelope.shape[1])


def solution(mesh):
    placed = (
        P(("walk", "row"), "col"),
        P("walk"),
        P("walk", None),
        P(),
        P(),
        P(),
        P(),
        P(),
        P(),
        P(None, "col"),
        P(("walk", "row"), "col"),
        P(("walk", "row"), "col"),
    )

    def run(*args):
        with jax.sharding.use_abstract_mesh(mesh.abstract_mesh):
            return jax.shard_map(
                per_device,
                mesh=mesh,
                in_specs=placed,
                out_specs=(P(("walk", "row"), "col"), P(("walk", "row"), "col")),
                check_vma=False,
            )(*args)

    return run
```
